256 devices in a mesh: ang: 128 (over x_lo, z, y, core), row: 2 (over x_hi).
Axes of the slice: x: 4 (x_hi: 2, x_lo: 2; x = x_hi * 2 + x_lo), y: 4, z: 8, core: 2. Of those that a mesh axis runs over, the one named last changes fastest.
Arguments:
- sample: bfloat16 [256, 20, 256, 128], P('ang', None, 'row')
- flat_speckle: bfloat16 [20, 256, 128], P(None, 'row')
- peak_shift: int32 [2, 256, 256, 128], P(None, 'ang', 'row'), may hold values from -2 to 2, as said below
- partner: int32 [256], P('ang'), may hold values from 0 to 255, as said below
Outputs:
- sinogram: float32 [2, 256, 256, 128], P(None, ('row', 'ang'))
The draws below stay inside these ranges and needn't reach their ends.
Inputs may be any that keep to these rules, and one draw needn't show every extreme that they name: partner[j] lies in the block of 2 projections that starts at ((j // 2 + 256 // 4) % 128) * 2, and partner[partner[j]] = j. peak_shift is the same on every pixel of an aligned tile of 4 x 4 pixels of one projection.
All inputs are finite; a program needn't handle non-finite values.
Results may differ from the reference program's by a relative error of at most 0.0003.
Values may be sent and summed in bfloat16 or wider, within the bound.
No kernel may reach another device: no remote copies, remote signals or barrier semaphores. Data moves between devices by JAX's collectives and lax.ppermute only.
A program may use at most 320 MiB of HBM per device.

```python
import jax
import jax.numpy as jnp
from jax import lax

CH = 20
EDGE = 128
CYCLE = 8
COLS = 128
PROJ_DEV = 2
ROWS = 256
NPROJ = 256


def draw_partner(key, part):
    blocks = NPROJ // PROJ_DEV
    half = blocks // 2
    keys = jax.random.split(jax.random.fold_in(key, 17), half)
    orders = jax.vmap(lambda single: jax.random.permutation(single, PROJ_DEV))(keys).astype(jnp.int32)
    inverse = jnp.argsort(orders, axis=1).astype(jnp.int32)
    block_ids = jnp.arange(half, dtype=jnp.int32)[:, None]
    first_half = (block_ids + half) * PROJ_DEV + orders
    second_half = block_ids * PROJ_DEV + inverse
    return jnp.concatenate([first_half.reshape(-1), second_half.reshape(-1)]).astype(jnp.int32)


def spread_tiles(values):
    return jnp.repeat(jnp.repeat(values, 4, axis=-2), 4, axis=-1)


def speckle_fields(key):
    flat_key = jax.random.fold_in(key, 101)
    shift_key = jax.random.fold_in(key, 202)
    flat = jax.random.normal(flat_key, (CH, ROWS, COLS), jnp.float32)
    flat = jnp.clip(flat, -6.0, 6.0)
    coarse = jax.random.randint(shift_key, (2, NPROJ, ROWS // 4, COLS // 4), -2, 3).astype(jnp.int32)
    return (flat, spread_tiles(coarse).astype(jnp.int32))


def draw_flat_speckle(key, part):
    flat, shifts = speckle_fields(key)
    return flat.astype(jnp.bfloat16)


def draw_peak_shift(key, part):
    flat, shifts = speckle_fields(key)
    return shifts


def draw_sample(key, part):
    flat, shifts = speckle_fields(key)
    frac_key = jax.random.fold_in(key, 303)
    noise_key = jax.random.fold_in(key, 404)
    gain_key = jax.random.fold_in(key, 505)
    row_grid = jnp.arange(ROWS, dtype=jnp.int32)[:, None] + jnp.zeros((1, COLS), jnp.int32)
    col_grid = jnp.arange(COLS, dtype=jnp.int32)[None, :] + jnp.zeros((ROWS, 1), jnp.int32)

    def one_image(index):
        frac = jax.random.uniform(jax.random.fold_in(frac_key, index), (2, ROWS // 4, COLS // 4), jnp.float32, 0.0, 0.5)
        frac = spread_tiles(frac)
        row_base = jnp.clip(row_grid + shifts[0, index], 0, ROWS - 1)
        row_next = jnp.clip(row_grid + shifts[0, index] + 1, 0, ROWS - 1)
        col_base = jnp.clip(col_grid + shifts[1, index], 0, COLS - 1)
        col_next = jnp.clip(col_grid + shifts[1, index] + 1, 0, COLS - 1)
        fr = frac[0]
        fc = frac[1]
        blended = (1.0 - fr) * (1.0 - fc) * flat[:, row_base, col_base] + (1.0 - fr) * fc * flat[:, row_base, col_next] + fr * (1.0 - fc) * flat[:, row_next, col_base] + fr * fc * flat[:, row_next, col_next]
        gain = spread_tiles(jax.random.uniform(jax.random.fold_in(gain_key, index), (ROWS // 4, COLS // 4), jnp.float32, 0.7, 1.3))
        noise = 0.3 * jax.random.normal(jax.random.fold_in(noise_key, index), (CH, ROWS, COLS), jnp.float32)
        image = jnp.clip(gain * blended + noise, -6.0, 6.0)
        return image.astype(jnp.bfloat16)
    return lax.map(one_image, jnp.arange(NPROJ, dtype=jnp.int32))


def setup_inputs(seed: int = 0) -> dict:
    streams_of = jax.random.split(jax.random.key(seed), 5)
    return {
        "sample": draw_sample(jax.random.fold_in(streams_of[4], 71), 0),
        "flat_speckle": draw_flat_speckle(jax.random.fold_in(streams_of[4], 71), 0),
        "peak_shift": draw_peak_shift(jax.random.fold_in(streams_of[4], 71), 0),
        "partner": draw_partner(jax.random.fold_in(streams_of[4], 71), 0),
    }


SHARPNESS = 12.0
EPSILON = 1e-05

def window_sum(values, axis):
    length = values.shape[axis] - 6
    total = lax.slice_in_dim(values, 0, length, axis=axis)
    for offset in range(1, 7):
        total = total + lax.slice_in_dim(values, offset, offset + length, axis=axis)
    return total

def box_window(values):
    return window_sum(window_sum(values, values.ndim - 2), values.ndim - 1)

def stitch(own_edge, far_edge):
    edge_cols = own_edge.shape[-1]
    position = jnp.arange(edge_cols).astype(jnp.float32)
    own_weight = (edge_cols - 0.5 - position) / edge_cols
    far_weight = (position + 0.5) / edge_cols
    blended = own_weight * own_edge.astype(jnp.float32) + far_weight * far_edge.astype(jnp.float32)
    return blended.astype(jnp.bfloat16)

def track(padded, flat_pad, energy_ref, shift_rows, shift_cols):
    rows = padded.shape[-2] - 6
    cols = padded.shape[-1] - 6
    energy = box_window(lax.optimization_barrier(jnp.sum(jnp.square(padded.astype(jnp.float32)), axis=-3)))
    total = jnp.zeros(energy.shape, jnp.float32)
    along_rows = jnp.zeros(energy.shape, jnp.float32)
    along_cols = jnp.zeros(energy.shape, jnp.float32)
    for row_shift in range(-3, 4):
        for col_shift in range(-3, 4):
            moved = lax.slice(flat_pad, (0, 3 + row_shift, 3 + col_shift), (flat_pad.shape[0], 3 + row_shift + rows + 6, 3 + col_shift + cols + 6))
            product = lax.optimization_barrier(jnp.sum(padded.astype(jnp.float32) * moved.astype(jnp.float32), axis=-3))
            window = box_window(product)
            energy_moved = lax.slice(energy_ref, (3 + row_shift, 3 + col_shift), (3 + row_shift + rows, 3 + col_shift + cols))
            score = window / jnp.sqrt((energy + EPSILON) * (energy_moved + EPSILON))
            off_rows = row_shift - shift_rows
            off_cols = col_shift - shift_cols
            inside = (jnp.abs(off_rows) <= 1) & (jnp.abs(off_cols) <= 1)
            weight = jnp.where(inside, jnp.exp(SHARPNESS * score), jnp.zeros(score.shape, score.dtype))
            total = total + weight
            along_rows = along_rows + weight * off_rows.astype(jnp.float32)
            along_cols = along_cols + weight * off_cols.astype(jnp.float32)
    grad_rows = shift_rows.astype(jnp.float32) + along_rows / total
    grad_cols = shift_cols.astype(jnp.float32) + along_cols / total
    return (grad_rows, grad_cols)

def smooth_columns(column_mean, half_width):
    cols = column_mean.shape[-1]
    padded_mean = jnp.pad(column_mean, ((0, 0), (0, 0), (0, 0), (half_width, half_width)))
    summed = lax.slice_in_dim(padded_mean, 0, cols, axis=3)
    for offset in range(1, 2 * half_width + 1):
        summed = summed + lax.slice_in_dim(padded_mean, offset, offset + cols, axis=3)
    position = jnp.arange(cols)
    counted = (jnp.minimum(position + half_width, cols - 1) - jnp.maximum(position - half_width, 0) + 1).astype(jnp.float32)
    return summed / counted

def apply_cycles(sinogram, column_mean):
    return sinogram - (column_mean - smooth_columns(column_mean, CYCLE))

def reference(sample, flat_speckle, peak_shift, partner):
    flat_pad = jnp.pad(flat_speckle, ((0, 0), (6, 6), (0, 0)))
    flat_pad = jnp.pad(flat_pad, ((0, 0), (0, 0), (6, 6)), mode='reflect')
    energy_ref = box_window(lax.optimization_barrier(jnp.sum(jnp.square(flat_pad.astype(jnp.float32)), axis=0)))

    def one_projection(item):
        index, mate = item
        image = sample[index]
        mate_edge = sample[mate][:, :, COLS - EDGE:]
        seam = stitch(image[:, :, COLS - EDGE:], jnp.flip(mate_edge, 2))
        stitched = jnp.concatenate([image[:, :, :COLS - EDGE], seam], axis=2)
        padded = jnp.pad(stitched, ((0, 0), (3, 3), (0, 0)))
        padded = jnp.pad(padded, ((0, 0), (0, 0), (3, 3)), mode='reflect')
        grad_rows, grad_cols = track(padded, flat_pad, energy_ref, peak_shift[0, index], peak_shift[1, index])
        return jnp.stack([grad_rows, grad_cols])
    grads = lax.map(one_projection, (jnp.arange(NPROJ).astype(jnp.int32), partner))
    sinogram = jnp.transpose(grads, (1, 2, 0, 3))
    column_mean = lax.optimization_barrier(jnp.sum(sinogram, axis=2, keepdims=True)) / NPROJ
    return apply_cycles(sinogram, column_mean)
```

```python
import functools

import jax
import jax.numpy as jnp
import numpy as np
from jax import lax
from jax.experimental import pallas as pl
from jax.experimental.pallas import tpu as pltpu
from jax.sharding import PartitionSpec as P

CYCLE = 8
SHARPNESS = 12.0
EPSILON = 1e-05

COLS = 128
CH = 20
SLAB = 72
HALO = 8
WIN = SLAB + HALO
HALF = 64
STEP = 9
SHIFTS = 7
HIGHEST = lax.Precision.HIGHEST


def reflect(position):
    position = np.abs(position)
    return np.where(position > COLS - 1, 2 * (COLS - 1) - position, position)


def column_tables():
    col = np.arange(COLS)
    shift = np.zeros((COLS, SHIFTS, COLS), np.float32)
    spread = np.zeros((COLS, SHIFTS, COLS), np.float32)
    for v in range(SHIFTS):
        shift[reflect(col + v - 3), v, col] = 1.0
        for k in range(-3, 4):
            np.add.at(spread, (reflect(col + v - 3 + k), v, col), 1.0)
    band = np.zeros((COLS, COLS), np.float32)
    edge = np.zeros((COLS, COLS), np.float32)
    for k in range(-3, 4):
        seen = col + k
        inside = (seen >= 0) & (seen < COLS)
        band[seen[inside], col[inside]] += 1.0
        edge[reflect(seen[~inside]), col[~inside]] += 1.0
    both = np.block([[band, edge], [edge, band]])
    zero = np.zeros_like(band)
    alone = np.block([[band + edge, zero], [zero, band + edge]])
    own = np.diag((COLS - 0.5 - col) / COLS)
    far = np.zeros((COLS, COLS))
    far[COLS - 1 - col, col] = (col + 0.5) / COLS
    seam = np.block([[own, far], [far, own]])
    flat = (COLS, SHIFTS * COLS)
    return shift.reshape(flat), spread.reshape(flat), both, alone, seam


def row_tables():
    box = np.zeros((88, WIN), np.float32)
    for row in range(3, WIN - 3):
        box[row, row - 3 : row + 4] = 1.0
    tiles = np.zeros((WIN, 16), np.float32)
    rows = np.arange(HALF)
    tiles[rows, rows // 4] = 1.0
    return box, tiles


def bf16(table):
    return jnp.asarray(table, jnp.bfloat16)


def prepare_kernel(meta, slab, halo, shift, spread, box, flats, norms):
    half = meta[0]
    slab_at = pl.multiple_of(8 * (1 - half), 8)
    halo_at = pl.multiple_of(SLAB * half, 8)
    for ch in range(CH):
        moved = jnp.dot(slab[ch], shift[...], preferred_element_type=jnp.float32)
        for v in range(SHIFTS):
            flats[v, ch, pl.ds(slab_at, SLAB), :] = moved[:, v * COLS : (v + 1) * COLS]
        moved = jnp.dot(halo[0, ch], shift[...], preferred_element_type=jnp.float32)
        for v in range(SHIFTS):
            flats[v, ch, pl.ds(halo_at, HALO), :] = moved[:, v * COLS : (v + 1) * COLS]
    squares = jnp.zeros((WIN, COLS), jnp.float32)
    for ch in range(CH):
        image = flats[3, ch]
        squares = squares + image * image
    rows = jnp.dot(box[...], squares, precision=HIGHEST, preferred_element_type=jnp.float32)
    energy = jnp.dot(rows, spread[...], precision=HIGHEST, preferred_element_type=jnp.float32)
    for v in range(SHIFTS):
        norms[v] = lax.rsqrt(energy[:, v * COLS : (v + 1) * COLS] + EPSILON)


def prepare(meta, slab, halo, shift, spread, box):
    vmem = pl.BlockSpec(memory_space=pltpu.VMEM)
    return pl.pallas_call(
        prepare_kernel,
        name="prepare",
        out_shape=(
            jax.ShapeDtypeStruct((SHIFTS, CH, WIN, COLS), jnp.float32),
            jax.ShapeDtypeStruct((SHIFTS, 88, COLS), jnp.float32),
        ),
        in_specs=[pl.BlockSpec(memory_space=pltpu.SMEM)] + [vmem] * 5,
        out_specs=(vmem, vmem),
    )(meta, slab, halo, shift, spread, box)


def split(values):
    high = values.astype(jnp.bfloat16)
    low = (values - high.astype(jnp.float32)).astype(jnp.bfloat16)
    return high, low


def box_rows(load):
    rows = [load(t) for t in range(STEP + 6)]
    pairs = [rows[i] + rows[i + 1] for i in range(STEP + 4)]
    fours = [pairs[i] + pairs[i + 2] for i in range(STEP)]
    return [(fours[t] + pairs[t + 4]) + rows[t + 6] for t in range(STEP)]


def track_kernel(
    order, meta, own, got, own_halo, got_halo, flats, norms, seam, both, alone, tiles, before,
    out, padded, peaks, products, squares, high, low, high0, low0, window, window0, staged,
):
    half = meta[0]
    slab_at = pl.multiple_of(8 * (1 - half), 8)
    halo_at = pl.multiple_of(SLAB * half, 8)

    def stitch(own_rows, got_rows, at, count):
        for ch in range(CH):
            rows = jnp.concatenate([own_rows(ch), got_rows(ch)], axis=1)
            blended = jnp.dot(rows, seam[...], preferred_element_type=jnp.float32)
            blended = blended.astype(jnp.bfloat16).astype(jnp.float32)
            padded[0, ch, pl.ds(at, count), :] = blended[:, :COLS]
            padded[1, ch, pl.ds(at, count), :] = blended[:, COLS:]

    stitch(lambda ch: own[0, ch], lambda ch: got[ch], slab_at, SLAB)
    stitch(lambda ch: own_halo[0, ch], lambda ch: got_halo[0, ch], halo_at, HALO)
    for d in range(2):
        for j, source in enumerate((own[0, CH, d * 16 : d * 16 + 16], got[CH, d * 16 : d * 16 + 16])):
            peaks[j, d] = jnp.dot(tiles[...], source, preferred_element_type=jnp.float32)

    def multiply(t, carry):
        for v in range(SHIFTS):
            sums = [[None, None] for _ in range(SHIFTS)]
            for ch in range(CH):
                image = [padded[j, ch, pl.ds(t + 5, 8, stride=STEP), :] for j in range(2)]
                for u in range(SHIFTS):
                    moved = flats[v, ch, pl.ds(t + 2 + u, 8, stride=STEP), :]
                    for j in range(2):
                        term = image[j] * moved
                        sums[u][j] = term if ch == 0 else sums[u][j] + term
            for u in range(SHIFTS):
                for j in range(2):
                    products[v, u, j, pl.ds(t, 8, stride=STEP), :] = sums[u][j]
        for j in range(2):
            total = None
            for ch in range(CH):
                image = padded[j, ch, pl.ds(t + 5, 8, stride=STEP), :]
                total = image * image if ch == 0 else total + image * image
            squares[j, pl.ds(t, 8, stride=STEP), :] = total
        return carry

    lax.fori_loop(0, STEP, multiply, 0)

    blank = jnp.zeros((8, COLS), jnp.float32)

    def box(u, carry):
        for v in range(SHIFTS):
            sums = [
                box_rows(lambda t, j=j: products[v, u, j, pl.ds(t, 8, stride=STEP), :]) for j in range(2)
            ]
            if v == 3:
                for j in range(2):
                    one, two = split(jnp.concatenate(sums[j] + [blank], axis=0))
                    at = pl.ds(pl.multiple_of(u * 80, 16), 80)
                    high0[at, j * COLS : (j + 1) * COLS] = one
                    low0[at, j * COLS : (j + 1) * COLS] = two
            else:
                one, two = split(jnp.concatenate(sums[0] + sums[1], axis=0))
                at = pl.ds(pl.multiple_of(u * 144, 16), 144)
                pair, side = (v, 0) if v < 3 else (6 - v, 1)
                high[pair, at, side * COLS : (side + 1) * COLS] = one
                low[pair, at, side * COLS : (side + 1) * COLS] = two
        return carry

    lax.fori_loop(0, SHIFTS, box, 0)
    for j in range(2):
        sums = box_rows(lambda t, j=j: squares[j, pl.ds(t, 8, stride=STEP), :])
        one, two = split(jnp.concatenate(sums + [blank], axis=0))
        high0[560:640, j * COLS : (j + 1) * COLS] = one
        low0[560:640, j * COLS : (j + 1) * COLS] = two

    for pair in range(3):
        window[pair] = jnp.dot(
            high[pair], both[...], preferred_element_type=jnp.float32
        ) + jnp.dot(low[pair], both[...], preferred_element_type=jnp.float32)
    window0[...] = jnp.dot(high0[...], alone[...], preferred_element_type=jnp.float32) + jnp.dot(
        low0[...], alone[...], preferred_element_type=jnp.float32
    )

    def choose(peak_is, candidates):
        chosen = candidates[4]
        for peak in range(4):
            chosen = jnp.where(peak_is[peak], candidates[peak], chosen)
        return chosen

    def score(t, carry):
        for j in range(2):
            peak = [peaks[j, d, pl.ds(t, 8, stride=STEP), :] for d in range(2)]
            row_is = [peak[0] == float(p - 2) for p in range(4)]
            col_is = [peak[1] == float(p - 2) for p in range(4)]
            at = pl.multiple_of(t * 8, 8)
            energy = window0[pl.ds(560 + at, 8), j * COLS : (j + 1) * COLS]
            scale = lax.rsqrt(energy + EPSILON) * SHARPNESS
            near = [[] for _ in range(3)]
            for v in range(SHIFTS):
                scaled = []
                for u in range(SHIFTS):
                    if v == 3:
                        value = window0[pl.ds(u * 80 + at, 8), j * COLS : (j + 1) * COLS]
                    else:
                        pair, side = (v, 0) if v < 3 else (6 - v, 1)
                        value = window[pair, pl.ds(u * 144 + j * 72 + at, 8), side * COLS : (side + 1) * COLS]
                    scaled.append(value * norms[v, pl.ds(t + 5 + u, 8, stride=STEP), :])
                for a in range(3):
                    near[a].append(choose(row_is, scaled[a : a + 5]))
            weight = [
                [jnp.exp(choose(col_is, near[a][b : b + 5]) * scale) for b in range(3)] for a in range(3)
            ]
            by_row = [(weight[a][0] + weight[a][1]) + weight[a][2] for a in range(3)]
            by_col = [(weight[0][b] + weight[1][b]) + weight[2][b] for b in range(3)]
            total = (by_row[0] + by_row[1]) + by_row[2]
            place = order[2 + j]
            staged[pl.ds(8 * t + place, 8, stride=8 * STEP), :] = peak[0] + (by_row[2] - by_row[0]) / total
            staged[pl.ds(8 * t + 4 + place, 8, stride=8 * STEP), :] = peak[1] + (by_col[2] - by_col[0]) / total
        return carry

    if before is not None:
        staged[0 : 8 * HALF, :] = before[...]
    lax.fori_loop(0, STEP, score, 0)
    out[...] = staged[0 : 8 * HALF, :]


def track(order, meta, own, got, own_halo, got_halo, tables, before, chunk):
    flats, norms, seam, both, alone, tiles = tables
    whole = lambda array: pl.BlockSpec(array.shape, lambda i, order, meta: (0,) * array.ndim)
    in_specs = [
        pl.BlockSpec((1, CH + 1, SLAB, COLS), lambda i, order, meta: (order[0], 0, 0, 0)),
        whole(got),
        pl.BlockSpec((1, CH, HALO, COLS), lambda i, order, meta: (order[0], 0, 0, 0)),
        pl.BlockSpec((1, CH, HALO, COLS), lambda i, order, meta: (chunk, 0, 0, 0)),
    ] + [whole(table) for table in tables]
    operands = [own, got, own_halo, got_halo, *tables]
    kernel = track_kernel
    if before is None:
        kernel = lambda *refs: track_kernel(*refs[:12], None, *refs[12:])
    else:
        in_specs.append(whole(before))
        operands.append(before)
    return pl.pallas_call(
        kernel,
        name="track",
        out_shape=jax.ShapeDtypeStruct((8 * HALF, COLS), jnp.float32),
        grid_spec=pltpu.PrefetchScalarGridSpec(
            num_scalar_prefetch=2,
            grid=(1,),
            in_specs=in_specs,
            out_specs=pl.BlockSpec((8 * HALF, COLS), lambda i, order, meta: (0, 0)),
            scratch_shapes=[
                pltpu.VMEM((2, CH, WIN, COLS), jnp.float32),
                pltpu.VMEM((2, 2, WIN, COLS), jnp.float32),
                pltpu.VMEM((SHIFTS, SHIFTS, 2, WIN, COLS), jnp.float32),
                pltpu.VMEM((2, WIN, COLS), jnp.float32),
                pltpu.VMEM((3, 1008, 2 * COLS), jnp.bfloat16),
                pltpu.VMEM((3, 1008, 2 * COLS), jnp.bfloat16),
                pltpu.VMEM((640, 2 * COLS), jnp.bfloat16),
                pltpu.VMEM((640, 2 * COLS), jnp.bfloat16),
                pltpu.VMEM((3, 1008, 2 * COLS), jnp.float32),
                pltpu.VMEM((640, 2 * COLS), jnp.float32),
                pltpu.VMEM((8 * SLAB, COLS), jnp.float32),
            ],
        ),
    )(order, meta, *operands)


def finish_kernel(total, sources, arrived, out):
    sums = arrived[0:8, :]
    for source in range(1, sources):
        sums = sums + arrived[8 * source : 8 * source + 8, :]
    col = lax.broadcasted_iota(jnp.int32, (8, COLS), 1)
    reach = jnp.minimum(col + CYCLE, COLS - 1) - jnp.maximum(col - CYCLE, 0) + 1
    for d in range(2):
        mean = jnp.sum(sums[4 * d : 4 * d + 4], axis=0, keepdims=True) / total
        mean = jnp.broadcast_to(mean, (8, COLS))
        smooth = mean
        for offset in range(1, CYCLE + 1):
            left = pltpu.roll(mean, offset, 1)
            right = pltpu.roll(mean, COLS - offset, 1)
            smooth = smooth + jnp.where(col >= offset, left, 0.0)
            smooth = smooth + jnp.where(col < COLS - offset, right, 0.0)
        ripple = mean - smooth / reach.astype(jnp.float32)
        for side in range(2):
            for q in range(2):
                for m in range(sources // 8):
                    rows = arrived[pl.ds(64 * m + 4 * d + 2 * side + q, 8, stride=8), :]
                    at = 2 * sources * side + 16 * m + q
                    out[d, pl.ds(at, 8, stride=2), :] = rows - ripple


def finish(arrived, projections):
    sources = projections // 4
    vmem = pl.BlockSpec(memory_space=pltpu.VMEM)
    return pl.pallas_call(
        functools.partial(finish_kernel, float(projections), sources),
        name="finish",
        out_shape=jax.ShapeDtypeStruct((2, projections, COLS), jnp.float32),
        in_specs=[vmem],
        out_specs=vmem,
    )(arrived)


def pack(sample, rows, peaks, part):
    slab = lax.dynamic_slice_in_dim(sample, rows, SLAB, axis=2)
    half_peaks = lax.dynamic_slice_in_dim(peaks, part * 16, 16, axis=2)
    half_peaks = jnp.transpose(half_peaks, (1, 0, 2, 3)).reshape(2, 1, 32, COLS)
    half_peaks = jnp.pad(half_peaks, ((0, 0), (0, 0), (0, SLAB - 32), (0, 0)))
    return jnp.concatenate([slab, half_peaks], axis=1)


def body(sample, flat_speckle, peak_shift, partner):
    ang = lax.axis_size("ang")
    pairs = ang // 2
    half = (lax.axis_index("ang") // pairs).astype(jnp.int32)
    swap = (partner[0] % 2).astype(jnp.int32)
    order = [jnp.where(half == 0, k, k ^ swap) for k in range(2)]
    peaks = peak_shift[:, :, ::4, :].astype(jnp.bfloat16)
    route = [(i, (i + pairs) % ang) for i in range(ang)]

    send = pack(sample, 56 * (1 - half), peaks, 1 - half)
    got = [
        lax.ppermute(lax.dynamic_index_in_dim(send, order[k], 0, keepdims=False), "ang", route)
        for k in range(2)
    ]
    border = jnp.concatenate([sample, flat_speckle[None]], axis=0)
    straight = [(2 * i, 2 * i + 1) for i in range(pairs)] + [(2 * i + 1, 2 * i) for i in range(pairs, ang)]
    own_halo = lax.ppermute(
        lax.dynamic_slice_in_dim(border, 120 * (1 - half), HALO, axis=2), ("ang", "row"), straight
    )
    across = [(2 * i, 2 * (i - pairs) + 1) for i in range(pairs, ang)]
    across = across + [(2 * i + 1, 2 * (i + pairs)) for i in range(pairs)]
    edge = lax.dynamic_slice_in_dim(sample, 120 * half, HALO, axis=2)
    edge = jnp.where(order[0] == 0, edge, edge[::-1])
    got_halo = lax.ppermute(edge, ("ang", "row"), across)

    own = pack(sample, 56 * half, peaks, half)
    meta = half[None]
    shift, spread, both, alone, seam = column_tables()
    box, tiles = row_tables()
    flat_slab = lax.dynamic_slice_in_dim(flat_speckle, 56 * half, SLAB, axis=1)
    flats, norms = prepare(
        meta, flat_slab, own_halo[2:], bf16(shift), jnp.asarray(spread), jnp.asarray(box)
    )
    tables = (flats, norms, bf16(seam), bf16(both), bf16(alone), bf16(tiles))
    grads = None
    for k in range(2):
        low, high = jnp.int32(k), 2 + (k ^ swap)
        places = jnp.where(half == 0, jnp.stack([low, high]), jnp.stack([high, low]))
        steer = jnp.concatenate([order[k][None], order[k][None], places]).astype(jnp.int32)
        grads = track(steer, meta, own, got[k], own_halo, got_halo, tables, grads, k)

    groups = [list(range(pairs)), list(range(pairs, ang))]
    arrived = lax.all_to_all(
        grads.reshape(HALF, 8, COLS), "ang", 0, 0, axis_index_groups=groups, tiled=True
    )
    projections = 2 * ang
    sinogram = finish(arrived.reshape(8 * HALF, COLS), projections)
    return sinogram.reshape(2, 1, projections, COLS)


def solution(mesh):
    in_specs = (
        P("ang", None, "row", None),
        P(None, "row", None),
        P(None, "ang", "row", None),
        P("ang"),
    )
    out_specs = P(None, ("row", "ang"), None, None)
    return jax.shard_map(body, mesh=mesh, in_specs=in_specs, out_specs=out_specs, check_vma=False)
```

```python
import functools

import jax
import jax.numpy as jnp
from jax import lax
from jax.experimental import pallas as pl
from jax.experimental.pallas import tpu as pltpu
from jax.sharding import PartitionSpec as P


CYCLE = 8
SHARPNESS = 12.0
EPSILON = 1e-05

COLS = 128
CH = 20
SLAB = 72
HALO = 8
WIN = SLAB + HALO
HALF = 64
STEP = 9
SHIFTS = 7
HIGHEST = lax.Precision.HIGHEST


SMEM = pl.BlockSpec(memory_space=pltpu.SMEM)
VMEM = pl.BlockSpec(memory_space=pltpu.VMEM)
HBM = pl.BlockSpec(memory_space=pltpu.HBM)


def pack_kernel(code, sample, flat, peaks, send_0, send_1, straight, across, tall, sems):
    half, swap = code[0] & 1, code[0] >> 1
    other = 1 - half
    first = half * swap
    slab_at = pl.multiple_of(56 * other, 8)
    halo_at = pl.multiple_of(120 * other, 8)
    edge_at = pl.multiple_of(120 * half, 8)
    tall_at = pl.multiple_of(HALF * other, 8)
    copies = [
        (peaks.at[:, :, pl.ds(tall_at, HALF), :], tall),
        (sample.at[:, :, pl.ds(halo_at, HALO), :], straight.at[0:2]),
        (flat.at[:, pl.ds(halo_at, HALO), :], straight.at[2]),
        (sample.at[first, :, pl.ds(slab_at, SLAB), :], send_0.at[0:CH]),
        (sample.at[1 - first, :, pl.ds(slab_at, SLAB), :], send_1.at[0:CH]),
        (sample.at[first, :, pl.ds(edge_at, HALO), :], across.at[0]),
        (sample.at[1 - first, :, pl.ds(edge_at, HALO), :], across.at[1]),
    ]
    copies = [pltpu.make_async_copy(a, b, sems.at[i]) for i, (a, b) in enumerate(copies)]
    for copy in copies:
        copy.start()
    copies[0].wait()
    for send, index in ((send_0, first), (send_1, 1 - first)):
        rows = [tall[d, index, pl.ds(0, 16, stride=4), :] for d in range(2)]
        rows = rows + [jnp.zeros((SLAB - 32, COLS), jnp.int32)]
        send[CH] = jnp.concatenate(rows, axis=0).astype(jnp.float32).astype(jnp.bfloat16)
    for copy in copies[1:]:
        copy.wait()


def pack(code, sample, flat, peaks):
    image = lambda *shape: jax.ShapeDtypeStruct((*shape, COLS), jnp.bfloat16)
    return pl.pallas_call(
        pack_kernel,
        name="pack",
        out_shape=(
            image(CH + 1, SLAB), image(CH + 1, SLAB), image(3, CH, HALO), image(2, CH, HALO),
        ),
        in_specs=[SMEM, HBM, HBM, HBM],
        out_specs=(VMEM,) * 4,
        scratch_shapes=[pltpu.VMEM((2, 2, HALF, COLS), jnp.int32), pltpu.SemaphoreType.DMA((7,))],
        compiler_params=pltpu.CompilerParams(vmem_limit_bytes=8 << 20),
    )(code, sample, flat, peaks)


def within(a, b, reach):
    return (jnp.abs(a - b) <= reach).astype(jnp.float32)


def seam_tables():
    r = lax.broadcasted_iota(jnp.int32, (COLS, COLS), 0)
    c = lax.broadcasted_iota(jnp.int32, (COLS, COLS), 1)
    last = COLS - 1
    own = jnp.where(r == c, (last - c).astype(jnp.float32) + 0.5, 0.0) / COLS
    far = jnp.where(r == last - c, c.astype(jnp.float32) + 0.5, 0.0) / COLS
    band = within(r, c, 3)
    edge = jnp.where(jnp.logical_and(r >= 1, r + c <= 3), 1.0, 0.0)
    edge = edge + jnp.where(jnp.logical_and(r <= last - 1, r + c >= 2 * last - 3), 1.0, 0.0)
    zero = jnp.zeros_like(band)

    def blocks(a, b):
        rows = [jnp.concatenate([a, b], axis=1), jnp.concatenate([b, a], axis=1)]
        return jnp.concatenate(rows, axis=0)

    return blocks(own, far), blocks(band, edge), blocks(band + edge, zero)


def prepare_kernel(
    code, flat_all, halo, sample, peaks, flats, norms, own, own_peaks, seam, both, alone, tiles, flat, sems
):
    half = code[0] & 1
    tall_at = pl.multiple_of(HALF * half, 8)
    from_row = pl.multiple_of(56 * half, 8)
    copies = [
        (flat_all.at[:, pl.ds(from_row, SLAB), :], flat),
        (sample.at[:, :, pl.ds(from_row, SLAB), :], own),
        (peaks.at[:, :, pl.ds(tall_at, HALF), :], own_peaks),
    ]
    copies = [pltpu.make_async_copy(a, b, sems.at[i]) for i, (a, b) in enumerate(copies)]
    for copy in copies:
        copy.start()
    for ref, table in zip((seam, both, alone), seam_tables()):
        ref[...] = table.astype(jnp.bfloat16)
    row = lax.broadcasted_iota(jnp.int32, (WIN, 16), 0)
    tile = lax.broadcasted_iota(jnp.int32, (WIN, 16), 1)
    tiles[...] = jnp.where(row >> 2 == tile, 1.0, 0.0).astype(jnp.bfloat16)
    slab_at = pl.multiple_of(8 * (1 - half), 8)
    halo_at = pl.multiple_of(SLAB * half, 8)
    last = COLS - 1
    source = lax.broadcasted_iota(jnp.int32, (COLS, COLS), 0)
    target = lax.broadcasted_iota(jnp.int32, (COLS, COLS), 1)
    shift, spread = [], []
    for v in range(-3, 4):
        seen = target + v
        low = jnp.where(source >= 1, -source, -COLS)
        high = jnp.where(source <= last - 1, 2 * last - source, 3 * COLS)
        for tables, reach in ((shift, 0), (spread, 3)):
            table = within(source, seen, reach) + within(low, seen, reach) + within(high, seen, reach)
            tables.append(table.astype(jnp.bfloat16))
    shift = jnp.concatenate(shift, axis=1)
    spread = jnp.concatenate(spread, axis=1)
    copies[0].wait()
    for ch in range(CH):
        moved = jnp.dot(flat[ch], shift, preferred_element_type=jnp.float32)
        for v in range(SHIFTS):
            flats[v, ch, pl.ds(slab_at, SLAB), :] = moved[:, v * COLS : (v + 1) * COLS]
        moved = jnp.dot(halo[2, ch], shift, preferred_element_type=jnp.float32)
        for v in range(SHIFTS):
            flats[v, ch, pl.ds(halo_at, HALO), :] = moved[:, v * COLS : (v + 1) * COLS]
    squares = jnp.zeros((WIN, COLS), jnp.float32)
    for ch in range(CH):
        image = flats[3, ch]
        squares = squares + image * image
    center = lax.broadcasted_iota(jnp.int32, (88, WIN), 0)
    member = lax.broadcasted_iota(jnp.int32, (88, WIN), 1)
    box = within(center, member, 3)
    rows = jnp.dot(box, squares, precision=HIGHEST, preferred_element_type=jnp.float32)
    high, low = split(rows)
    energy = jnp.dot(high, spread, preferred_element_type=jnp.float32) + jnp.dot(
        low, spread, preferred_element_type=jnp.float32
    )
    for v in range(SHIFTS):
        norms[v] = lax.rsqrt(energy[:, v * COLS : (v + 1) * COLS] + EPSILON)
    copies[1].wait()
    copies[2].wait()


def prepare(code, flat, halo, sample, peaks):
    table = lambda *shape: jax.ShapeDtypeStruct(shape, jnp.bfloat16)
    return pl.pallas_call(
        prepare_kernel,
        name="prepare",
        out_shape=(
            jax.ShapeDtypeStruct((SHIFTS, CH, WIN, COLS), jnp.float32),
            jax.ShapeDtypeStruct((SHIFTS, 88, COLS), jnp.float32),
            table(2, CH, SLAB, COLS),
            jax.ShapeDtypeStruct((2, 2, HALF, COLS), jnp.int32),
            table(2 * COLS, 2 * COLS),
            table(2 * COLS, 2 * COLS),
            table(2 * COLS, 2 * COLS),
            table(WIN, 16),
        ),
        in_specs=[SMEM, HBM, VMEM, HBM, HBM],
        out_specs=(VMEM,) * 8,
        scratch_shapes=[pltpu.VMEM((CH, SLAB, COLS), jnp.bfloat16), pltpu.SemaphoreType.DMA((3,))],
        compiler_params=pltpu.CompilerParams(vmem_limit_bytes=16 << 20),
    )(code, flat, halo, sample, peaks)


def split(values):
    high = values.astype(jnp.bfloat16)
    low = (values - high.astype(jnp.float32)).astype(jnp.bfloat16)
    return high, low


def box_rows(load):
    rows = [load(t) for t in range(STEP + 6)]
    pairs = [rows[i] + rows[i + 1] for i in range(STEP + 4)]
    fours = [pairs[i] + pairs[i + 2] for i in range(STEP)]
    return [(fours[t] + pairs[t + 4]) + rows[t + 6] for t in range(STEP)]


def track_kernel(
    chunk, code, own, own_peaks, got, own_halo, got_halo, flats, norms, seam, both, alone, tiles, before,
    out, padded, peaks, products, squares, high, low, high0, low0, window, window0, staged,
):
    half, swap = code[0] & 1, code[0] >> 1
    swapped = chunk ^ swap
    index = jnp.where(half == 0, chunk, swapped)
    places = (jnp.where(half == 0, chunk, 2 + swapped), jnp.where(half == 0, 2 + swapped, chunk))
    slab_at = pl.multiple_of(8 * (1 - half), 8)
    halo_at = pl.multiple_of(SLAB * half, 8)

    def stitch(own_rows, got_rows, at, count):
        for ch in range(CH):
            rows = jnp.concatenate([own_rows(ch), got_rows(ch)], axis=1)
            blended = jnp.dot(rows, seam[...], preferred_element_type=jnp.float32)
            blended = blended.astype(jnp.bfloat16).astype(jnp.float32)
            padded[0, ch, pl.ds(at, count), :] = blended[:, :COLS]
            padded[1, ch, pl.ds(at, count), :] = blended[:, COLS:]

    stitch(lambda ch: own[index, ch], lambda ch: got[ch], slab_at, SLAB)
    stitch(lambda ch: own_halo[index, ch], lambda ch: got_halo[chunk, ch], halo_at, HALO)
    for d in range(2):
        tall = own_peaks[d, index]
        peaks[0, d, 0:HALF, :] = tall.astype(jnp.float32)
        peaks[0, d, HALF:WIN, :] = jnp.zeros((WIN - HALF, COLS), jnp.float32)
        source = got[CH, d * 16 : d * 16 + 16]
        peaks[1, d] = jnp.dot(tiles[...], source, preferred_element_type=jnp.float32)

    def multiply(t, carry):
        for v in range(SHIFTS):
            sums = [[None, None] for _ in range(SHIFTS)]
            for ch in range(CH):
                image = [padded[j, ch, pl.ds(t + 5, 8, stride=STEP), :] for j in range(2)]
                for u in range(SHIFTS):
                    moved = flats[v, ch, pl.ds(t + 2 + u, 8, stride=STEP), :]
                    for j in range(2):
                        term = image[j] * moved
                        sums[u][j] = term if ch == 0 else sums[u][j] + term
            for u in range(SHIFTS):
                for j in range(2):
                    products[v, u, j, pl.ds(t, 8, stride=STEP), :] = sums[u][j]
        for j in range(2):
            total = None
            for ch in range(CH):
                image = padded[j, ch, pl.ds(t + 5, 8, stride=STEP), :]
                total = image * image if ch == 0 else total + image * image
            squares[j, pl.ds(t, 8, stride=STEP), :] = total
        return carry

    lax.fori_loop(0, STEP, multiply, 0)

    blank = jnp.zeros((8, COLS), jnp.float32)

    def box(u, carry):
        for v in range(SHIFTS):
            sums = [
                box_rows(lambda t, j=j: products[v, u, j, pl.ds(t, 8, stride=STEP), :]) for j in range(2)
            ]
            if v == 3:
                for j in range(2):
                    one, two = split(jnp.concatenate(sums[j] + [blank], axis=0))
                    at = pl.ds(pl.multiple_of(u * 80, 16), 80)
                    high0[at, j * COLS : (j + 1) * COLS] = one
                    low0[at, j * COLS : (j + 1) * COLS] = two
            else:
                one, two = split(jnp.concatenate(sums[0] + sums[1], axis=0))
                at = pl.ds(pl.multiple_of(u * 144, 16), 144)
                pair, side = (v, 0) if v < 3 else (6 - v, 1)
                high[pair, at, side * COLS : (side + 1) * COLS] = one
                low[pair, at, side * COLS : (side + 1) * COLS] = two
        return carry

    lax.fori_loop(0, SHIFTS, box, 0)
    for j in range(2):
        sums = box_rows(lambda t, j=j: squares[j, pl.ds(t, 8, stride=STEP), :])
        one, two = split(jnp.concatenate(sums + [blank], axis=0))
        high0[560:640, j * COLS : (j + 1) * COLS] = one
        low0[560:640, j * COLS : (j + 1) * COLS] = two

    for pair in range(3):
        window[pair] = jnp.dot(
            high[pair], both[...], preferred_element_type=jnp.float32
        ) + jnp.dot(low[pair], both[...], preferred_element_type=jnp.float32)
    window0[...] = jnp.dot(high0[...], alone[...], preferred_element_type=jnp.float32) + jnp.dot(
        low0[...], alone[...], preferred_element_type=jnp.float32
    )

    def choose(peak_is, candidates):
        chosen = candidates[4]
        for peak in range(4):
            chosen = jnp.where(peak_is[peak], candidates[peak], chosen)
        return chosen

    def score(t, carry):
        for j in range(2):
            peak = [peaks[j, d, pl.ds(t, 8, stride=STEP), :] for d in range(2)]
            row_is = [peak[0] == float(p - 2) for p in range(4)]
            col_is = [peak[1] == float(p - 2) for p in range(4)]
            at = pl.multiple_of(t * 8, 8)
            energy = window0[pl.ds(560 + at, 8), j * COLS : (j + 1) * COLS]
            scale = lax.rsqrt(energy + EPSILON) * SHARPNESS
            near = [[] for _ in range(3)]
            for v in range(SHIFTS):
                scaled = []
                for u in range(SHIFTS):
                    if v == 3:
                        value = window0[pl.ds(u * 80 + at, 8), j * COLS : (j + 1) * COLS]
                    else:
                        pair, side = (v, 0) if v < 3 else (6 - v, 1)
                        value = window[pair, pl.ds(u * 144 + j * 72 + at, 8), side * COLS : (side + 1) * COLS]
                    scaled.append(value * norms[v, pl.ds(t + 5 + u, 8, stride=STEP), :])
                for a in range(3):
                    near[a].append(choose(row_is, scaled[a : a + 5]))
            weight = [
                [jnp.exp(choose(col_is, near[a][b : b + 5]) * scale) for b in range(3)] for a in range(3)
            ]
            by_row = [(weight[a][0] + weight[a][1]) + weight[a][2] for a in range(3)]
            by_col = [(weight[0][b] + weight[1][b]) + weight[2][b] for b in range(3)]
            total = (by_row[0] + by_row[1]) + by_row[2]
            place = places[j]
            staged[pl.ds(8 * t + place, 8, stride=8 * STEP), :] = peak[0] + (by_row[2] - by_row[0]) / total
            staged[pl.ds(8 * t + 4 + place, 8, stride=8 * STEP), :] = peak[1] + (by_col[2] - by_col[0]) / total
        return carry

    if before is not None:
        staged[0 : 8 * HALF, :] = before[...]
    lax.fori_loop(0, STEP, score, 0)
    out[...] = staged[0 : 8 * HALF, :]


def track(chunk, code, own, own_peaks, got, own_halo, got_halo, tables, before):
    operands = [code, own, own_peaks, got, own_halo, got_halo, *tables]
    if before is None:
        kernel = lambda *refs: track_kernel(chunk, *refs[:12], None, *refs[12:])
    else:
        kernel = functools.partial(track_kernel, chunk)
        operands.append(before)
    return pl.pallas_call(
        kernel,
        name="track",
        out_shape=jax.ShapeDtypeStruct((8 * HALF, COLS), jnp.float32),
        in_specs=[SMEM] + [VMEM] * (len(operands) - 1),
        out_specs=VMEM,
        scratch_shapes=[
            pltpu.VMEM((2, CH, WIN, COLS), jnp.float32),
            pltpu.VMEM((2, 2, WIN, COLS), jnp.float32),
            pltpu.VMEM((SHIFTS, SHIFTS, 2, WIN, COLS), jnp.float32),
            pltpu.VMEM((2, WIN, COLS), jnp.float32),
            pltpu.VMEM((3, 1008, 2 * COLS), jnp.bfloat16),
            pltpu.VMEM((3, 1008, 2 * COLS), jnp.bfloat16),
            pltpu.VMEM((640, 2 * COLS), jnp.bfloat16),
            pltpu.VMEM((640, 2 * COLS), jnp.bfloat16),
            pltpu.VMEM((3, 1008, 2 * COLS), jnp.float32),
            pltpu.VMEM((640, 2 * COLS), jnp.float32),
            pltpu.VMEM((8 * SLAB, COLS), jnp.float32),
        ],
        compiler_params=pltpu.CompilerParams(vmem_limit_bytes=24 << 20),
    )(*operands)


def finish_kernel(total, sources, arrived, out):
    sums = arrived[0:8, :]
    for source in range(1, sources):
        sums = sums + arrived[8 * source : 8 * source + 8, :]
    col = lax.broadcasted_iota(jnp.int32, (8, COLS), 1)
    reach = jnp.minimum(col + CYCLE, COLS - 1) - jnp.maximum(col - CYCLE, 0) + 1
    for d in range(2):
        mean = jnp.sum(sums[4 * d : 4 * d + 4], axis=0, keepdims=True) / total
        mean = jnp.broadcast_to(mean, (8, COLS))
        smooth = mean
        for offset in range(1, CYCLE + 1):
            left = pltpu.roll(mean, offset, 1)
            right = pltpu.roll(mean, COLS - offset, 1)
            smooth = smooth + jnp.where(col >= offset, left, 0.0)
            smooth = smooth + jnp.where(col < COLS - offset, right, 0.0)
        ripple = mean - smooth / reach.astype(jnp.float32)
        for side in range(2):
            for q in range(2):
                for m in range(sources // 8):
                    rows = arrived[pl.ds(64 * m + 4 * d + 2 * side + q, 8, stride=8), :]
                    at = 2 * sources * side + 16 * m + q
                    out[d, pl.ds(at, 8, stride=2), :] = rows - ripple


def finish(arrived, projections):
    sources = projections // 4
    return pl.pallas_call(
        functools.partial(finish_kernel, float(projections), sources),
        name="finish",
        out_shape=jax.ShapeDtypeStruct((2, projections, COLS), jnp.float32),
        in_specs=[VMEM],
        out_specs=VMEM,
        compiler_params=pltpu.CompilerParams(vmem_limit_bytes=8 << 20),
    )(arrived)


def program(sample, flat_speckle, peak_shift, partner):
    ang = lax.axis_size("ang")
    pairs = ang // 2
    half = (lax.axis_index("ang") >= pairs).astype(jnp.int32)
    route = [(i, (i + pairs) % ang) for i in range(ang)]
    straight = [(2 * i, 2 * i + 1) for i in range(pairs)] + [(2 * i + 1, 2 * i) for i in range(pairs, ang)]
    across = [(2 * i, 2 * (i - pairs) + 1) for i in range(pairs, ang)]
    across = across + [(2 * i + 1, 2 * (i + pairs)) for i in range(pairs)]

    code = (half + 2 * (partner[0] & 1))[None]
    sample, flat_speckle, peak_shift = (
        pltpu.with_memory_space_constraint(array, pltpu.HBM) for array in (sample, flat_speckle, peak_shift)
    )
    send_0, send_1, straight_rows, across_rows = pack(code, sample, flat_speckle, peak_shift)
    own_halo = lax.ppermute(straight_rows, ("ang", "row"), straight)
    got_0 = lax.ppermute(send_0, "ang", route)
    got_halo = lax.ppermute(across_rows, ("ang", "row"), across)
    got_1 = lax.ppermute(send_1, "ang", route)

    flats, norms, own, own_peaks, *tables = prepare(code, flat_speckle, own_halo, sample, peak_shift)
    tables = (flats, norms, *tables)
    grads = None
    for k, got in enumerate((got_0, got_1)):
        grads = track(k, code, own, own_peaks, got, own_halo, got_halo, tables, grads)

    groups = [list(range(pairs)), list(range(pairs, ang))]
    arrived = lax.all_to_all(
        grads.reshape(HALF, 8, COLS), "ang", 0, 0, axis_index_groups=groups, tiled=True
    )
    projections = 2 * ang
    sinogram = finish(arrived.reshape(8 * HALF, COLS), projections)
    return sinogram.reshape(2, 1, projections, COLS)


def solution(mesh):
    in_specs = (
        P("ang", None, "row", None),
        P(None, "row", None),
        P(None, "ang", "row", None),
        P("ang"),
    )
    out_specs = P(None, ("row", "ang"), None, None)
    return jax.shard_map(program, mesh=mesh, in_specs=in_specs, out_specs=out_specs, check_vma=False)
```

```python
import functools

import jax
import jax.numpy as jnp
from jax import lax
from jax.experimental import pallas as pl
from jax.experimental.pallas import tpu as pltpu
from jax.sharding import PartitionSpec as P


CYCLE = 8
SHARPNESS = 12.0
EPSILON = 1e-05

COLS = 128
CH = 20
SLAB = 72
HALO = 8
WIN = SLAB + HALO
HALF = 64
STEP = 9
SHIFTS = 7
HIGHEST = lax.Precision.HIGHEST


SMEM = pl.BlockSpec(memory_space=pltpu.SMEM)
VMEM = pl.BlockSpec(memory_space=pltpu.VMEM)
HBM = pl.BlockSpec(memory_space=pltpu.HBM)


def fill(send, tall, index):
    rows = [tall[d, index, pl.ds(0, 16, stride=4), :] for d in range(2)]
    rows = rows + [jnp.zeros((SLAB - 32, COLS), jnp.int32)]
    send[CH] = jnp.concatenate(rows, axis=0).astype(jnp.float32).astype(jnp.bfloat16)


def begin(copies, sems):
    copies = [pltpu.make_async_copy(a, b, sems.at[i]) for i, (a, b) in enumerate(copies)]
    for copy in copies:
        copy.start()
    return copies


def pack_first_kernel(code, sample, peaks, send, tall, sems):
    half, swap = code[0] & 1, code[0] >> 1
    other = 1 - half
    index = half * swap
    slab_at = pl.multiple_of(56 * other, 8)
    tall_at = pl.multiple_of(HALF * other, 8)
    copies = begin(
        [
            (peaks.at[:, :, pl.ds(tall_at, HALF), :], tall),
            (sample.at[index, :, pl.ds(slab_at, SLAB), :], send.at[0:CH]),
        ],
        sems,
    )
    copies[0].wait()
    fill(send, tall, index)
    copies[1].wait()


def pack_rest_kernel(
    code, sample, flat, peaks, send, straight, across, flat_slab, tall, near, far, sems
):
    half, swap = code[0] & 1, code[0] >> 1
    other = 1 - half
    index = 1 - half * swap
    slab_at = pl.multiple_of(56 * other, 8)
    tall_at = pl.multiple_of(HALF * other, 8)
    near_at = pl.multiple_of(120 * other, 8)
    far_at = pl.multiple_of(120 * half, 8)
    own_at = pl.multiple_of(56 * half, 8)
    copies = begin(
        [
            (peaks.at[:, :, pl.ds(tall_at, HALF), :], tall),
            (sample.at[:, :, pl.ds(near_at, HALO), :], near),
            (sample.at[:, :, pl.ds(far_at, HALO), :], far),
            (flat.at[:, pl.ds(far_at, HALO), :], across.at[CH : 2 * CH]),
            (sample.at[index, :, pl.ds(slab_at, SLAB), :], send.at[0:CH]),
            (flat.at[:, pl.ds(own_at, SLAB), :], flat_slab),
        ],
        sems,
    )
    copies[0].wait()
    fill(send, tall, index)
    copies[1].wait()
    copies[2].wait()
    for source, target, upper, select in ((near, straight, half, None), (far, across, other, index)):
        for j in range(2):
            which = j if select is None else (select ^ 1 ^ j)
            for m in range(CH // 2):
                one = source[which, m].astype(jnp.float32)
                two = source[which, m + CH // 2].astype(jnp.float32)
                top = jnp.concatenate([one[0:4], two[0:4]], axis=0)
                bottom = jnp.concatenate([one[4:8], two[4:8]], axis=0)
                tile = jnp.where(upper == 1, top, bottom)
                target[j * (CH // 2) + m] = tile.astype(jnp.bfloat16)
    for copy in copies[3:]:
        copy.wait()


def image(*shape):
    return jax.ShapeDtypeStruct((*shape, COLS), jnp.bfloat16)


def pack_first(code, sample, peaks):
    return pl.pallas_call(
        pack_first_kernel,
        name="pack_first",
        out_shape=image(CH + 1, SLAB),
        in_specs=[SMEM, HBM, HBM],
        out_specs=VMEM,
        scratch_shapes=[pltpu.VMEM((2, 2, HALF, COLS), jnp.int32), pltpu.SemaphoreType.DMA((2,))],
        compiler_params=pltpu.CompilerParams(vmem_limit_bytes=8 << 20),
    )(code, sample, peaks)


def pack_rest(code, sample, flat, peaks):
    return pl.pallas_call(
        pack_rest_kernel,
        name="pack_rest",
        out_shape=(image(CH + 1, SLAB), image(CH, HALO), image(2 * CH, HALO), image(CH, SLAB)),
        in_specs=[SMEM, HBM, HBM, HBM],
        out_specs=(VMEM,) * 4,
        scratch_shapes=[
            pltpu.VMEM((2, 2, HALF, COLS), jnp.int32),
            pltpu.VMEM((2, CH, HALO, COLS), jnp.bfloat16),
            pltpu.VMEM((2, CH, HALO, COLS), jnp.bfloat16),
            pltpu.SemaphoreType.DMA((6,)),
        ],
        compiler_params=pltpu.CompilerParams(vmem_limit_bytes=8 << 20),
    )(code, sample, flat, peaks)


def within(a, b, reach):
    return (jnp.abs(a - b) <= reach).astype(jnp.float32)


def seam_tables():
    r = lax.broadcasted_iota(jnp.int32, (COLS, COLS), 0)
    c = lax.broadcasted_iota(jnp.int32, (COLS, COLS), 1)
    last = COLS - 1
    own = jnp.where(r == c, (last - c).astype(jnp.float32) + 0.5, 0.0) / COLS
    far = jnp.where(r == last - c, c.astype(jnp.float32) + 0.5, 0.0) / COLS
    band = within(r, c, 3)
    edge = jnp.where(jnp.logical_and(r >= 1, r + c <= 3), 1.0, 0.0)
    edge = edge + jnp.where(jnp.logical_and(r <= last - 1, r + c >= 2 * last - 3), 1.0, 0.0)
    zero = jnp.zeros_like(band)

    def blocks(a, b):
        rows = [jnp.concatenate([a, b], axis=1), jnp.concatenate([b, a], axis=1)]
        return jnp.concatenate(rows, axis=0)

    both, alone = blocks(band, edge), blocks(band + edge, zero)
    twice = lambda table: jnp.concatenate([table, table], axis=0)
    return blocks(own, far), twice(both), twice(alone)


def prepare_kernel(
    code, flat, halo, sample, peaks, flats, norms, own, own_peaks, seam, both, alone, tiles, framed, sems
):
    half = code[0] & 1
    tall_at = pl.multiple_of(HALF * half, 8)
    from_row = pl.multiple_of(56 * half, 8)
    slab_at = pl.multiple_of(8 * (1 - half), 8)
    halo_at = pl.multiple_of(SLAB * half, 8)
    copies = [
        (flat, framed.at[:, pl.ds(slab_at, SLAB), :]),
        (halo.at[CH : 2 * CH], framed.at[:, pl.ds(halo_at, HALO), :]),
        (sample.at[:, :, pl.ds(from_row, SLAB), :], own),
        (peaks.at[:, :, pl.ds(tall_at, HALF), :], own_peaks),
    ]
    copies = begin(copies, sems)
    for ref, table in zip((seam, both, alone), seam_tables()):
        ref[...] = table.astype(jnp.bfloat16)
    row = lax.broadcasted_iota(jnp.int32, (WIN, 16), 0)
    tile = lax.broadcasted_iota(jnp.int32, (WIN, 16), 1)
    tiles[...] = jnp.where(row >> 2 == tile, 1.0, 0.0).astype(jnp.bfloat16)
    last = COLS - 1
    source = lax.broadcasted_iota(jnp.int32, (COLS, COLS), 0)
    target = lax.broadcasted_iota(jnp.int32, (COLS, COLS), 1)
    shift, spread = [], []
    for v in range(-3, 4):
        seen = target + v
        low = jnp.where(source >= 1, -source, -COLS)
        high = jnp.where(source <= last - 1, 2 * last - source, 3 * COLS)
        for tables, reach in ((shift, 0), (spread, 3)):
            table = within(source, seen, reach) + within(low, seen, reach) + within(high, seen, reach)
            tables.append(table.astype(jnp.bfloat16))
    spread = jnp.concatenate(spread, axis=1)
    copies[0].wait()
    copies[1].wait()
    rows = framed[...].reshape(CH * WIN, COLS)
    for v in range(0, SHIFTS, 2):
        table = jnp.concatenate(shift[v : v + 2], axis=1)
        moved = jnp.dot(rows, table, preferred_element_type=jnp.float32)
        for side in range(table.shape[1] // COLS):
            part = moved[:, side * COLS : (side + 1) * COLS]
            flats[v + side] = part.reshape(CH, WIN, COLS)
    squares = jnp.zeros((WIN, COLS), jnp.float32)
    for ch in range(CH):
        image = flats[3, ch]
        squares = squares + image * image
    center = lax.broadcasted_iota(jnp.int32, (88, WIN), 0)
    member = lax.broadcasted_iota(jnp.int32, (88, WIN), 1)
    box = within(center, member, 3)
    rows = jnp.dot(box, squares, precision=HIGHEST, preferred_element_type=jnp.float32)
    high, low = split(rows)
    energy = jnp.dot(high, spread, preferred_element_type=jnp.float32) + jnp.dot(
        low, spread, preferred_element_type=jnp.float32
    )
    for v in range(SHIFTS):
        norms[v] = lax.rsqrt(energy[:, v * COLS : (v + 1) * COLS] + EPSILON)
    for copy in copies[2:]:
        copy.wait()


def prepare(code, flat, halo, sample, peaks):
    table = lambda *shape: jax.ShapeDtypeStruct(shape, jnp.bfloat16)
    return pl.pallas_call(
        prepare_kernel,
        name="prepare",
        out_shape=(
            jax.ShapeDtypeStruct((SHIFTS, CH, WIN, COLS), jnp.float32),
            jax.ShapeDtypeStruct((SHIFTS, 88, COLS), jnp.float32),
            table(2, CH, SLAB, COLS),
            jax.ShapeDtypeStruct((2, 2, HALF, COLS), jnp.int32),
            table(2 * COLS, 2 * COLS),
            table(4 * COLS, 2 * COLS),
            table(4 * COLS, 2 * COLS),
            table(WIN, 16),
        ),
        in_specs=[SMEM, VMEM, VMEM, HBM, HBM],
        out_specs=(VMEM,) * 8,
        scratch_shapes=[pltpu.VMEM((CH, WIN, COLS), jnp.bfloat16), pltpu.SemaphoreType.DMA((4,))],
        compiler_params=pltpu.CompilerParams(vmem_limit_bytes=16 << 20),
    )(code, flat, halo, sample, peaks)


def split(values):
    high = values.astype(jnp.bfloat16)
    low = (values - high.astype(jnp.float32)).astype(jnp.bfloat16)
    return high, low


def box_rows(load):
    rows = [load(t) for t in range(STEP + 6)]
    pairs = [rows[i] + rows[i + 1] for i in range(STEP + 4)]
    fours = [pairs[i] + pairs[i + 2] for i in range(STEP)]
    return [(fours[t] + pairs[t + 4]) + rows[t + 6] for t in range(STEP)]


def track_kernel(
    chunk, code, own, own_peaks, got, own_halo, got_halo, flats, norms, seam, both, alone, tiles, before,
    out, padded, peaks, products, squares, boxed_a, boxed_b, boxed0_a, boxed0_b, window, window0, staged,
):
    half, swap = code[0] & 1, code[0] >> 1
    swapped = chunk ^ swap
    index = jnp.where(half == 0, chunk, swapped)
    places = (jnp.where(half == 0, chunk, 2 + swapped), jnp.where(half == 0, 2 + swapped, chunk))
    slab_at = pl.multiple_of(8 * (1 - half), 8)
    halo_at = pl.multiple_of(4 + (SLAB - 4) * half, 4)

    def stitch(own_rows, got_rows):
        rows = jnp.concatenate([own_rows, got_rows], axis=1)
        blended = jnp.dot(rows, seam[...], preferred_element_type=jnp.float32)
        blended = blended.astype(jnp.bfloat16).astype(jnp.float32)
        return blended[:, :COLS], blended[:, COLS:]

    for ch in range(CH):
        for j, rows in enumerate(stitch(own[index, ch], got[ch])):
            padded[j, ch, pl.ds(slab_at, SLAB), :] = rows
    for m in range(CH // 2):
        tiles_of = (own_halo[index * (CH // 2) + m], got_halo[chunk * (CH // 2) + m])
        for j, rows in enumerate(stitch(*tiles_of)):
            padded[j, m, pl.ds(halo_at, 4), :] = rows[0:4]
            padded[j, m + CH // 2, pl.ds(halo_at, 4), :] = rows[4:8]
    for d in range(2):
        tall = own_peaks[d, index]
        peaks[0, d, 0:HALF, :] = tall.astype(jnp.float32)
        peaks[0, d, HALF:WIN, :] = jnp.zeros((WIN - HALF, COLS), jnp.float32)
        source = got[CH, d * 16 : d * 16 + 16]
        peaks[1, d] = jnp.dot(tiles[...], source, preferred_element_type=jnp.float32)

    def multiply(t, carry):
        for v in range(SHIFTS):
            sums = [[None, None] for _ in range(SHIFTS)]
            for ch in range(CH):
                image = [padded[j, ch, pl.ds(t + 5, 8, stride=STEP), :] for j in range(2)]
                for u in range(SHIFTS):
                    moved = flats[v, ch, pl.ds(t + 2 + u, 8, stride=STEP), :]
                    for j in range(2):
                        term = image[j] * moved
                        sums[u][j] = term if ch == 0 else sums[u][j] + term
            for u in range(SHIFTS):
                for j in range(2):
                    products[v, u, j, pl.ds(t, 8, stride=STEP), :] = sums[u][j]
        for j in range(2):
            total = None
            for ch in range(CH):
                image = padded[j, ch, pl.ds(t + 5, 8, stride=STEP), :]
                total = image * image if ch == 0 else total + image * image
            squares[j, pl.ds(t, 8, stride=STEP), :] = total
        return carry

    lax.fori_loop(0, STEP, multiply, 0)

    blank = jnp.zeros((8, COLS), jnp.float32)

    def sums(v, u, j):
        return box_rows(lambda t: products[v, u, j, pl.ds(t, 8, stride=STEP), :])

    def store(ref, at, left, right):
        for side, part in enumerate((left, right)):
            values = jnp.concatenate(part, axis=0)
            for place, piece in zip((side, side + 2), split(values)):
                ref[at : at + values.shape[0], place * COLS : (place + 1) * COLS] = piece

    def box(u, slot):
        for pair in range(3):
            left, right = (sums(v, u, 0) + sums(v, u, 1) for v in (pair, 6 - pair))
            store(boxed[slot], pair * 144, left, right)
        store(boxed0[slot], 0, sums(3, u, 0) + [blank], sums(3, u, 1) + [blank])

    def widen(u, slot):
        found = jnp.dot(boxed[slot][...], both[...], preferred_element_type=jnp.float32)
        for pair in range(3):
            at = pl.ds(pl.multiple_of(u * 144, 16), 144)
            window[pair, at, :] = found[pair * 144 : (pair + 1) * 144]
        at = pl.ds(pl.multiple_of(u * 80, 16), 80)
        window0[at, :] = jnp.dot(boxed0[slot][...], alone[...], preferred_element_type=jnp.float32)

    boxed, boxed0 = (boxed_a, boxed_b), (boxed0_a, boxed0_b)
    box(0, 0)

    def box_next(i, carry):
        u = 2 * i
        widen(u, 0)
        box(u + 1, 1)
        widen(u + 1, 1)
        box(u + 2, 0)
        return carry

    for i in range(SHIFTS // 2):
        box_next(i, 0)
    left, right = (
        box_rows(lambda t, j=j: squares[j, pl.ds(t, 8, stride=STEP), :]) + [blank] for j in range(2)
    )
    store(boxed0_b, 0, left, right)
    widen(SHIFTS - 1, 0)
    window0[560:640, :] = jnp.dot(boxed0_b[...], alone[...], preferred_element_type=jnp.float32)

    def choose(peak_is, candidates):
        chosen = candidates[4]
        for peak in range(4):
            chosen = jnp.where(peak_is[peak], candidates[peak], chosen)
        return chosen

    def score(t, carry):
        for j in range(2):
            peak = [peaks[j, d, pl.ds(t, 8, stride=STEP), :] for d in range(2)]
            row_is = [peak[0] == float(p - 2) for p in range(4)]
            col_is = [peak[1] == float(p - 2) for p in range(4)]
            at = pl.multiple_of(t * 8, 8)
            energy = window0[pl.ds(560 + at, 8), j * COLS : (j + 1) * COLS]
            scale = lax.rsqrt(energy + EPSILON) * SHARPNESS
            near = [[] for _ in range(3)]
            for v in range(SHIFTS):
                scaled = []
                for u in range(SHIFTS):
                    if v == 3:
                        value = window0[pl.ds(u * 80 + at, 8), j * COLS : (j + 1) * COLS]
                    else:
                        pair, side = (v, 0) if v < 3 else (6 - v, 1)
                        value = window[pair, pl.ds(u * 144 + j * 72 + at, 8), side * COLS : (side + 1) * COLS]
                    scaled.append(value * norms[v, pl.ds(t + 5 + u, 8, stride=STEP), :])
                for a in range(3):
                    near[a].append(choose(row_is, scaled[a : a + 5]))
            weight = [
                [jnp.exp(choose(col_is, near[a][b : b + 5]) * scale) for b in range(3)] for a in range(3)
            ]
            by_row = [(weight[a][0] + weight[a][1]) + weight[a][2] for a in range(3)]
            by_col = [(weight[0][b] + weight[1][b]) + weight[2][b] for b in range(3)]
            total = (by_row[0] + by_row[1]) + by_row[2]
            place = places[j]
            staged[pl.ds(8 * t + place, 8, stride=8 * STEP), :] = peak[0] + (by_row[2] - by_row[0]) / total
            staged[pl.ds(8 * t + 4 + place, 8, stride=8 * STEP), :] = peak[1] + (by_col[2] - by_col[0]) / total
        return carry

    if before is not None:
        staged[0 : 8 * HALF, :] = before[...]
    lax.fori_loop(0, STEP, score, 0, unroll=3)
    out[...] = staged[0 : 8 * HALF, :]


def track(chunk, code, own, own_peaks, got, own_halo, got_halo, tables, before):
    operands = [code, own, own_peaks, got, own_halo, got_halo, *tables]
    if before is None:
        kernel = lambda *refs: track_kernel(chunk, *refs[:12], None, *refs[12:])
    else:
        kernel = functools.partial(track_kernel, chunk)
        operands.append(before)
    return pl.pallas_call(
        kernel,
        name="track",
        out_shape=jax.ShapeDtypeStruct((8 * HALF, COLS), jnp.float32),
        in_specs=[SMEM] + [VMEM] * (len(operands) - 1),
        out_specs=VMEM,
        scratch_shapes=[
            pltpu.VMEM((2, CH, WIN, COLS), jnp.float32),
            pltpu.VMEM((2, 2, WIN, COLS), jnp.float32),
            pltpu.VMEM((SHIFTS, SHIFTS, 2, WIN, COLS), jnp.float32),
            pltpu.VMEM((2, WIN, COLS), jnp.float32),
            pltpu.VMEM((432, 4 * COLS), jnp.bfloat16),
            pltpu.VMEM((432, 4 * COLS), jnp.bfloat16),
            pltpu.VMEM((80, 4 * COLS), jnp.bfloat16),
            pltpu.VMEM((80, 4 * COLS), jnp.bfloat16),
            pltpu.VMEM((3, 1008, 2 * COLS), jnp.float32),
            pltpu.VMEM((640, 2 * COLS), jnp.float32),
            pltpu.VMEM((8 * SLAB, COLS), jnp.float32),
        ],
        compiler_params=pltpu.CompilerParams(vmem_limit_bytes=24 << 20),
    )(*operands)


def finish_kernel(total, sources, arrived, out):
    sums = arrived[0:8, :]
    for source in range(1, sources):
        sums = sums + arrived[8 * source : 8 * source + 8, :]
    col = lax.broadcasted_iota(jnp.int32, (8, COLS), 1)
    reach = jnp.minimum(col + CYCLE, COLS - 1) - jnp.maximum(col - CYCLE, 0) + 1
    for d in range(2):
        mean = jnp.sum(sums[4 * d : 4 * d + 4], axis=0, keepdims=True) / total
        mean = jnp.broadcast_to(mean, (8, COLS))
        smooth = mean
        for offset in range(1, CYCLE + 1):
            left = pltpu.roll(mean, offset, 1)
            right = pltpu.roll(mean, COLS - offset, 1)
            smooth = smooth + jnp.where(col >= offset, left, 0.0)
            smooth = smooth + jnp.where(col < COLS - offset, right, 0.0)
        ripple = mean - smooth / reach.astype(jnp.float32)
        for side in range(2):
            for q in range(2):
                for m in range(sources // 8):
                    rows = arrived[pl.ds(64 * m + 4 * d + 2 * side + q, 8, stride=8), :]
                    at = 2 * sources * side + 16 * m + q
                    out[d, pl.ds(at, 8, stride=2), :] = rows - ripple


def finish(arrived, projections):
    sources = projections // 4
    return pl.pallas_call(
        functools.partial(finish_kernel, float(projections), sources),
        name="finish",
        out_shape=jax.ShapeDtypeStruct((2, projections, COLS), jnp.float32),
        in_specs=[VMEM],
        out_specs=VMEM,
        compiler_params=pltpu.CompilerParams(vmem_limit_bytes=8 << 20),
    )(arrived)


def program(sample, flat_speckle, peak_shift, partner):
    ang = lax.axis_size("ang")
    pairs = ang // 2
    half = (lax.axis_index("ang") >= pairs).astype(jnp.int32)
    route = [(i, (i + pairs) % ang) for i in range(ang)]
    straight = [(2 * i, 2 * i + 1) for i in range(pairs)] + [(2 * i + 1, 2 * i) for i in range(pairs, ang)]
    across = [(2 * i, 2 * (i - pairs) + 1) for i in range(pairs, ang)]
    across = across + [(2 * i + 1, 2 * (i + pairs)) for i in range(pairs)]

    code = (half + 2 * (partner[0] & 1))[None]
    sample, flat_speckle, peak_shift = (
        pltpu.with_memory_space_constraint(array, pltpu.HBM) for array in (sample, flat_speckle, peak_shift)
    )
    send_0 = pack_first(code, sample, peak_shift)
    got_0 = lax.ppermute(send_0, "ang", route)
    send_1, straight_rows, across_rows, flat_slab = pack_rest(code, sample, flat_speckle, peak_shift)
    got_halo = lax.ppermute(across_rows, ("ang", "row"), across)
    own_halo = lax.ppermute(straight_rows, ("ang", "row"), straight)
    got_1 = lax.ppermute(send_1, "ang", route)

    flats, norms, own, own_peaks, *tables = prepare(code, flat_slab, got_halo, sample, peak_shift)
    tables = (flats, norms, *tables)
    grads = None
    for k, got in enumerate((got_0, got_1)):
        grads = track(k, code, own, own_peaks, got, own_halo, got_halo, tables, grads)

    groups = [list(range(pairs)), list(range(pairs, ang))]
    arrived = lax.all_to_all(
        grads.reshape(HALF, 8, COLS), "ang", 0, 0, axis_index_groups=groups, tiled=True
    )
    projections = 2 * ang
    sinogram = finish(arrived.reshape(8 * HALF, COLS), projections)
    return sinogram.reshape(2, 1, projections, COLS)


def solution(mesh):
    in_specs = (
        P("ang", None, "row", None),
        P(None, "row", None),
        P(None, "ang", "row", None),
        P("ang"),
    )
    out_specs = P(None, ("row", "ang"), None, None)
    return jax.shard_map(program, mesh=mesh, in_specs=in_specs, out_specs=out_specs, check_vma=False)
```
